32 devices in a mesh: ctx: 16 (over z, y, x), ch: 2 (over core).
Axes of the slice: x: 2, y: 2, z: 4, core: 2. Of those that a mesh axis runs over, the one named last changes fastest.
Arguments:
- signal: bfloat16 [4096, 512], P('ctx', 'ch'), may hold values from -6 to 6
- gating: bfloat16 [4096, 512], P('ctx', 'ch'), may hold values from -6 to 6
- filter_taps: bfloat16 [4096], P('ctx'), may hold values from -4 to 4
- cotangent: bfloat16 [4096, 512], P('ctx', 'ch'), may hold values from -6 to 6
Outputs:
- grad_signal: bfloat16 [4096, 512], P('ctx', 'ch')
- grad_gating: bfloat16 [4096, 512], P('ctx', 'ch')
- grad_taps: float32 [4096], P('ctx')
The draws below stay inside these ranges and needn't reach their ends.
All inputs are finite; a program needn't handle non-finite values.
Results may differ from the reference program's by a relative error of at most 0.0069.
Values may be sent and summed in bfloat16 or wider, within the bound.
A program may use at most 64 MiB of HBM per device.

```python
import math
import jax
import jax.numpy as jnp
from jax import lax

CHANNELS = 512
BLOCK = 256
BLOCKS = 16
SEQUENCE_LENGTH = 4096


def draw_filter_taps(key, part):
    subkeys = jax.random.split(key, 5)
    step_floats = jnp.arange(SEQUENCE_LENGTH, dtype=jnp.int32).astype(jnp.float32)
    random_jitter = jnp.clip(jax.random.normal(subkeys[0], (SEQUENCE_LENGTH,), jnp.float32), -4.0, 4.0)
    fast_scale = jax.random.uniform(subkeys[1], (), jnp.float32, 0.2, 0.3) * BLOCK
    slow_scale = jax.random.uniform(subkeys[2], (), jnp.float32, 0.5, 2.0) * SEQUENCE_LENGTH
    split_positions = jax.random.randint(subkeys[3], (3,), 0, SEQUENCE_LENGTH)
    decline_amounts = jax.random.uniform(subkeys[4], (3,), jnp.float32, 0.5, 0.8)
    fast_share = 0.3
    fast_amp = jnp.sqrt(2.0 * fast_share / fast_scale)
    slow_total = (1.0 - jnp.exp(-2.0 * SEQUENCE_LENGTH / slow_scale)) / (1.0 - jnp.exp(-2.0 / slow_scale))
    slow_amp = jnp.sqrt((1.0 - fast_share) / slow_total)
    slow_amplitude_curve = slow_amp * jnp.exp(-step_floats / slow_scale)
    amplitude_curve = fast_amp * jnp.exp(-step_floats / fast_scale) + slow_amplitude_curve
    spike_events = jnp.ones((SEQUENCE_LENGTH,), jnp.float32)
    for selected_choice in range(3):
        spike_events = spike_events * jnp.where(step_floats >= split_positions[selected_choice].astype(jnp.float32), decline_amounts[selected_choice], 1.0)
    filter_coefficients = random_jitter * amplitude_curve * spike_events
    return filter_coefficients.astype(jnp.bfloat16)


def level_of(stream_key, dims, cuts, low, largest):
    factor_of = 1.0
    for position, parts in cuts:
        steps = jax.random.uniform(jax.random.fold_in(jax.random.fold_in(stream_key, 6), position), (parts,), jnp.float32, low / len(cuts), largest / len(cuts))
        factor_of = factor_of * jnp.repeat(jnp.exp(steps), dims[position] // parts).reshape((-1,) + (1,) * (len(dims) - 1 - position))
    return factor_of


def gaussian(own_key, extent, scale, reach, pieces=(), held_as=jnp.bfloat16):
    values = scale * jax.random.normal(own_key, extent, jnp.float32)
    if pieces:
        values = values * level_of(own_key, extent, pieces, -0.22, 0.18)
    return jnp.clip(values, -reach, reach).astype(held_as)


def setup_inputs(seed: int = 0) -> dict:
    key_of = jax.random.split(jax.random.key(seed), 5)
    signal = gaussian(key_of[0], (SEQUENCE_LENGTH, CHANNELS), 1.0, 6.0, ((0, 16), (1, 2)))
    gating = gaussian(key_of[1], (SEQUENCE_LENGTH, CHANNELS), 1.0, 6.0, ((0, 16), (1, 2)))
    filter_taps = draw_filter_taps(jax.random.fold_in(key_of[4], 71), 0)
    cotangent = gaussian(key_of[3], (SEQUENCE_LENGTH, CHANNELS), 1.0, 6.0, ((0, 16), (1, 2)))
    return dict(signal=signal, gating=gating, filter_taps=filter_taps, cotangent=cotangent)


highest = lax.Precision.HIGHEST

def build_tables(block_len):
    positions = jnp.arange(block_len, dtype=jnp.int32)
    period_len = 2 * block_len
    early_phase = positions[:, None] * positions[None, :] % period_len
    late_phase = (positions[:, None] + block_len) * positions[None, :] % period_len
    early_angle = early_phase.astype(jnp.float32) * (math.pi / block_len)
    late_angle = late_phase.astype(jnp.float32) * (math.pi / block_len)
    weight = jnp.where(positions == 0, 1.0, 2.0).astype(jnp.float32)
    sign_row = jnp.where(positions % 2 == 0, 1.0, -1.0).astype(jnp.float32)
    forward_cos = jnp.cos(early_angle).astype(jnp.bfloat16)
    forward_sin = (-jnp.sin(early_angle)).astype(jnp.bfloat16)
    early_cos = weight[None, :] * jnp.cos(early_angle)
    early_sin = -weight[None, :] * jnp.sin(early_angle)
    late_cos = weight[None, :] * jnp.cos(late_angle)
    late_sin = -weight[None, :] * jnp.sin(late_angle)
    return (forward_cos, forward_sin, early_cos, early_sin, late_cos, late_sin, sign_row)

def rounded(values):
    return lax.optimization_barrier(values.astype(jnp.bfloat16)).astype(jnp.float32)

def column_spectra(blocks, tables):
    forward_cos = tables[0].astype(jnp.float32)
    forward_sin = tables[1].astype(jnp.float32)
    values = blocks.astype(jnp.float32)
    real_part = jnp.einsum('fn,knc->kfc', forward_cos, values, precision=highest)
    imag_part = jnp.einsum('fn,knc->kfc', forward_sin, values, precision=highest)
    nyquist = jnp.einsum('n,knc->kc', tables[6], values, precision=highest)[:, None, :]
    return (real_part, imag_part, nyquist)

def earlier_blocks(member):
    return jnp.concatenate([jnp.zeros_like(member[:1]), member[:-1]], axis=0)

def pair_sums(v_spec, d_spec, f_spec, block_count):
    low_pad = tuple((jnp.concatenate([jnp.zeros_like(member), member], axis=0) for member in v_spec))
    high_pad = tuple((jnp.concatenate([member, jnp.zeros_like(member)], axis=0) for member in d_spec))

    def accumulate(running, offset):
        f_re, f_im, f_nyq = (lax.dynamic_slice_in_dim(member, offset, 1, 0) for member in f_spec)
        v_re, v_im, v_nyq = (lax.dynamic_slice_in_dim(member, block_count - offset, block_count, 0) for member in low_pad)
        d_re, d_im, d_nyq = (lax.dynamic_slice_in_dim(member, offset, block_count, 0) for member in high_pad)
        updated = (running[0] + f_re * v_re - f_im * v_im, running[1] + f_re * v_im + f_im * v_re, running[2] + f_nyq * v_nyq, running[3] + f_re * d_re + f_im * d_im, running[4] + f_re * d_im - f_im * d_re, running[5] + f_nyq * d_nyq)
        return (updated, None)
    initial = tuple((jnp.zeros_like(member) for member in v_spec + v_spec))
    totals, unused = lax.scan(accumulate, initial, jnp.arange(block_count, dtype=jnp.int32))
    return totals

def lag_sums(v_spec, d_spec, block_count, block_len):
    high_pad = tuple((jnp.concatenate([member, jnp.zeros_like(member)], axis=0) for member in d_spec))

    def accumulate(running, anchor):
        d_re, d_im, d_nyq = (lax.dynamic_slice_in_dim(member, anchor, block_count, 0) for member in high_pad)
        v_re, v_im, v_nyq = (lax.dynamic_slice_in_dim(member, anchor, 1, 0) for member in v_spec)
        updated = (running[0] + lax.optimization_barrier(jnp.sum(d_re * v_re + d_im * v_im, axis=2)), running[1] + lax.optimization_barrier(jnp.sum(d_im * v_re - d_re * v_im, axis=2)), running[2] + lax.optimization_barrier(jnp.sum(d_nyq * v_nyq, axis=2)))
        return (updated, None)
    initial = (jnp.zeros((block_count, block_len), jnp.float32), jnp.zeros((block_count, block_len), jnp.float32), jnp.zeros((block_count, 1), jnp.float32))
    totals, unused = lax.scan(accumulate, initial, jnp.arange(block_count, dtype=jnp.int32))
    return totals

def inverse_signal(real_part, imag_part, nyquist, cos_table, sin_table, sign_row, block_len):
    output = jnp.einsum('tf,kfc->ktc', rounded(cos_table), rounded(real_part), precision=highest)
    output = output + jnp.einsum('tf,kfc->ktc', rounded(sin_table), rounded(imag_part), precision=highest)
    return (output + sign_row[None, :, None] * nyquist) / (2.0 * block_len)

def inverse_taps(real_part, imag_part, nyquist, cos_table, sin_table, sign_row, block_len):
    output = jnp.einsum('tf,kf->kt', cos_table, real_part, precision=highest)
    output = output + jnp.einsum('tf,kf->kt', sin_table, imag_part, precision=highest)
    return (output + sign_row[None, :] * nyquist) / (2.0 * block_len)

def reference(signal, gating, filter_taps, cotangent):
    tables = build_tables(BLOCK)
    sign_row = tables[6]
    flip_col = sign_row[None, :, None]
    grad_mid = (cotangent.astype(jnp.float32) * gating.astype(jnp.float32)).astype(jnp.bfloat16)
    v_spec = column_spectra(signal.reshape(BLOCKS, BLOCK, CHANNELS), tables)
    d_raw = column_spectra(grad_mid.reshape(BLOCKS, BLOCK, CHANNELS), tables)
    d_spec = (d_raw[0] * flip_col, d_raw[1] * flip_col, d_raw[2])
    g_spec = column_spectra(filter_taps.reshape(BLOCKS, BLOCK, 1), tables)
    f_spec = (earlier_blocks(g_spec[0]) + flip_col * g_spec[0], earlier_blocks(g_spec[1]) + flip_col * g_spec[1], earlier_blocks(g_spec[2]) + g_spec[2])
    totals = pair_sums(v_spec, d_spec, f_spec, BLOCKS)
    recomputed = inverse_signal(totals[0], totals[1], totals[2], tables[4], tables[5], sign_row, BLOCK)
    recomputed = recomputed.reshape(SEQUENCE_LENGTH, CHANNELS)
    grad_gating = (cotangent.astype(jnp.float32) * recomputed).astype(jnp.bfloat16)
    grad_signal = inverse_signal(totals[3], totals[4], totals[5], tables[2], tables[3], sign_row, BLOCK)
    grad_signal = grad_signal.reshape(SEQUENCE_LENGTH, CHANNELS).astype(jnp.bfloat16)
    lag_re, lag_im, lag_nyq = lag_sums(v_spec, d_spec, BLOCKS, BLOCK)
    upper_half = inverse_taps(lag_re, lag_im, lag_nyq, tables[4], tables[5], sign_row, BLOCK)
    lower_half = inverse_taps(lag_re, lag_im, lag_nyq, tables[2], tables[3], sign_row, BLOCK)
    following = jnp.concatenate([lower_half[1:], jnp.zeros_like(lower_half[:1])], axis=0)
    grad_taps = ((upper_half + following) / math.sqrt(CHANNELS * SEQUENCE_LENGTH)).reshape(SEQUENCE_LENGTH)
    return (grad_signal, grad_gating, grad_taps)
```

```python
import functools
import math

import jax
import jax.numpy as jnp
from jax import lax
from jax.experimental import pallas as pl
from jax.experimental.pallas import tpu as pltpu
from jax.sharding import PartitionSpec as P

ROWS = 16
f32 = jnp.float32
bf16 = jnp.bfloat16


def kernel(
    n, cpd, norm,
    signal_ref, gating_ref, taps_ref, cot_ref,
    gs_ref, gg_ref, gt_ref,
    vsend, gsend, xpad, gpad, ysend, bsend, yret, bret,
    taps_all, hpad, toep, acc, xt_ref, mlag, merge, lagsend, lagrecv, lagsum, lagother,
    s_v, r_v, s_g, r_g, s_y, r_y, s_b, r_b, s_t, r_t, s_l, r_l, s_c, r_c,
):
    block, width = signal_ref.shape
    total = n * ROWS
    me = lax.axis_index("ctx")
    mate = 1 - lax.axis_index("ch")
    pieces = lax.axis_size("ch")

    barrier = pltpu.get_barrier_semaphore()

    def greet(d, _):
        pl.semaphore_signal(barrier, inc=1, device_id={"ctx": lax.rem(me + d, n)})
        return 0

    lax.fori_loop(1, n, greet, 0)
    if pieces == 2:
        pl.semaphore_signal(barrier, inc=1, device_id={"ch": mate})

    def split(rows_value, dst):
        if cpd == ROWS:
            dst[...] = rows_value.astype(bf16).reshape(n, ROWS, block)
        else:
            for p in range(n):
                part = rows_value[p * cpd : (p + 1) * cpd]
                pad = jnp.zeros((ROWS - cpd, block), f32)
                dst[p] = jnp.concatenate([part, pad], axis=0).astype(bf16)

    def joined(src):
        if cpd == ROWS:
            return src[...].reshape(width, block).astype(f32)
        for p in range(n):
            merge[p * cpd : (p + 1) * cpd, :] = src[p].astype(f32)[:cpd]
        return merge[...]

    def copy(src, dst, send, recv, p, where):
        return pltpu.make_async_remote_copy(
            src_ref=src, dst_ref=dst, send_sem=send.at[p], recv_sem=recv.at[where],
            device_id={"ctx": p},
        )

    def send_all(src, dst, base, send, recv):
        def step(d, _):
            p = lax.rem(me + d, n)
            copy(src.at[p], dst.at[base + me], send, recv, p, me).start()
            return 0

        lax.fori_loop(1, n, step, 0)

    def wait_recv(src, dst, base, send, recv):
        def step(d, _):
            p = lax.rem(me + n - d, n)
            copy(src.at[p], dst.at[base + p], send, recv, p, p).wait_recv()
            return 0

        lax.fori_loop(1, n, step, 0)

    def wait_send(src, dst, base, send, recv):
        def step(d, _):
            p = lax.rem(me + d, n)
            copy(src.at[p], dst.at[base + me], send, recv, p, me).wait_send()
            return 0

        lax.fori_loop(1, n, step, 0)

    split(signal_ref[...].astype(f32).T, vsend)
    own_taps = taps_ref[...]
    for p in range(n):
        lagrecv[p] = jnp.zeros((1, block), f32)
    taps_send = lagsum
    taps_send[...] = own_taps
    pl.semaphore_wait(barrier, n - 1 + (pieces - 1))

    def taps_step(d, _):
        p = lax.rem(me + d, n)
        copy(taps_send, taps_all.at[me], s_t, r_t, p, me).start()
        return 0

    lax.fori_loop(1, n, taps_step, 0)
    send_all(vsend, xpad, n, s_v, r_v)
    grad_mid = (cot_ref[...].astype(f32) * gating_ref[...].astype(f32)).astype(bf16)
    split(grad_mid.astype(f32).T, gsend)
    send_all(gsend, gpad, 0, s_g, r_g)

    xpad[pl.ds(n + me, 1)] = vsend[pl.ds(me, 1)]
    gpad[pl.ds(me, 1)] = gsend[pl.ds(me, 1)]
    taps_all[pl.ds(me, 1)] = own_taps[None]
    gpad[n:] = jnp.zeros((n, ROWS, block), bf16)
    if n > 16:
        xpad[:n] = jnp.zeros((n, ROWS, block), bf16)

    def taps_wait(d, _):
        p = lax.rem(me + n - d, n)
        copy(taps_send, taps_all.at[p], s_t, r_t, p, p).wait_recv()
        return 0

    lax.fori_loop(1, n, taps_wait, 0)

    def taps_sent(d, _):
        p = lax.rem(me + d, n)
        copy(taps_send, taps_all.at[me], s_t, r_t, p, me).wait_send()
        return 0

    lax.fori_loop(1, n, taps_sent, 0)

    half = block // 2
    hpad[:, :block] = jnp.zeros((1, block), f32)
    for j in range(n):
        hpad[:, (j + 1) * block : (j + 2) * block] = taps_all[j]
    toep[:, :block] = jnp.zeros((half, block), bf16)
    for j in range(1, n + 1):
        window = jnp.broadcast_to(hpad[:, j * block - half : (j + 1) * block], (half, block + half))
        turned = pltpu.roll(window, 0, 1, stride=1, stride_axis=0)
        toep[:, j * block : (j + 1) * block] = turned[:, half:].astype(bf16)

    def at(k):
        return k * block if isinstance(k, int) else pl.multiple_of(k * block, block)

    def table(k):
        upper = toep[:, pl.ds(at(k) + block, block)]
        lower = toep[:, pl.ds(at(k) + half, block)]
        return jnp.concatenate([upper, lower], axis=0)

    def over_blocks(step):
        if n <= 16:
            for k in range(n):
                step(k)
        else:
            lax.fori_loop(0, n, lambda k, _: (step(k), 0)[1], 0)

    nt = (((1,), (1,)), ((), ()))

    def forward_step(k):
        if isinstance(k, int):
            term = jnp.dot(
                xpad[n : 2 * n - k].reshape(total - k * ROWS, block), table(k),
                preferred_element_type=f32,
            ).reshape(n - k, ROWS, block)
            if k == 0:
                acc[...] = term
            else:
                acc[k:] += term
        else:
            acc[...] += jnp.dot(
                xpad[pl.ds(n - k, n)].reshape(total, block), table(k), preferred_element_type=f32
            ).reshape(n, ROWS, block)

    def backward_step(k):
        if isinstance(k, int):
            term = lax.dot_general(
                gpad[k:n].reshape(total - k * ROWS, block), table(k), nt,
                preferred_element_type=f32,
            ).reshape(n - k, ROWS, block)
            if k == 0:
                acc[...] = term
            else:
                acc[: n - k] += term
        else:
            acc[...] += lax.dot_general(
                gpad[pl.ds(k, n)].reshape(total, block), table(k), nt, preferred_element_type=f32
            ).reshape(n, ROWS, block)

    wait_recv(vsend, xpad, n, s_v, r_v)
    if n > 16:
        acc[...] = jnp.zeros((n, ROWS, block), f32)
    over_blocks(forward_step)
    ysend[...] = acc[...].astype(bf16)
    send_all(ysend, yret, 0, s_y, r_y)
    yret[pl.ds(me, 1)] = ysend[pl.ds(me, 1)]
    xt_ref[...] = xpad[n:].reshape(total, block).astype(f32).T.astype(bf16)

    wait_recv(gsend, gpad, 0, s_g, r_g)
    if n > 16:
        acc[...] = jnp.zeros((n, ROWS, block), f32)
    over_blocks(backward_step)
    bsend[...] = acc[...].astype(bf16)
    send_all(bsend, bret, 0, s_b, r_b)
    bret[pl.ds(me, 1)] = bsend[pl.ds(me, 1)]

    def lag_step(k):
        mlag[:, pl.ds(at(k), block)] = jnp.dot(
            xt_ref[...], gpad[pl.ds(k, n)].reshape(total, block), preferred_element_type=f32
        )

    over_blocks(lag_step)
    mlag[:, n * block :] = jnp.zeros((block, block), f32)

    def fold(c):
        start = at(2 * c)
        span = 2 * block + half
        part = mlag[:half, pl.ds(start, span)] + jnp.concatenate(
            [mlag[half:, pl.ds(start + half, 2 * block)], mlag[half:, pl.ds(start + half + 2 * block, half)]],
            axis=1,
        )
        size = half
        while size > 8:
            size //= 2
            part = part[:size] + pltpu.roll(part[size:], span - size, 1)
        while size > 1:
            size //= 2
            part = part + pltpu.roll(pltpu.roll(part, 8 - size, 0), span - size, 1)
        lagsend[2 * c] = part[:1, :block]
        lagsend[2 * c + 1] = part[:1, block : 2 * block]

    if n <= 16:
        for c in range(n // 2):
            fold(c)
    else:
        lax.fori_loop(0, n // 2, lambda c, _: (fold(c), 0)[1], 0)

    send_all(lagsend, lagrecv, 0, s_l, r_l)
    lagrecv[pl.ds(me, 1)] = lagsend[pl.ds(me, 1)]

    wait_recv(ysend, yret, 0, s_y, r_y)
    recomputed = joined(yret).T
    gg_ref[...] = (cot_ref[...].astype(f32) * recomputed).astype(bf16)

    wait_recv(lagsend, lagrecv, 0, s_l, r_l)
    lagsum[...] = jnp.sum(lagrecv[...], axis=0)
    if pieces == 2:
        swap = pltpu.make_async_remote_copy(
            src_ref=lagsum, dst_ref=lagother, send_sem=s_c, recv_sem=r_c, device_id={"ch": mate}
        )
        swap.start()

    wait_recv(bsend, bret, 0, s_b, r_b)
    gs_ref[...] = joined(bret).T.astype(bf16)
    if pieces == 2:
        swap.wait()
        gt_ref[...] = (lagsum[...] + lagother[...]) * norm
    else:
        gt_ref[...] = lagsum[...] * norm
    wait_send(vsend, xpad, n, s_v, r_v)
    wait_send(gsend, gpad, 0, s_g, r_g)
    wait_send(ysend, yret, 0, s_y, r_y)
    wait_send(bsend, bret, 0, s_b, r_b)
    wait_send(lagsend, lagrecv, 0, s_l, r_l)


def body(signal, gating, filter_taps, cotangent):
    block, width = signal.shape
    n = lax.axis_size("ctx")
    cpd = width // n
    norm = 1.0 / math.sqrt(width * lax.axis_size("ch") * block * n)
    chunk = (n, ROWS, block)
    vmem = pl.BlockSpec(memory_space=pltpu.VMEM)
    dma = pltpu.SemaphoreType.DMA
    grad_signal, grad_gating, grad_taps = pl.pallas_call(
        functools.partial(kernel, n, cpd, norm),
        out_shape=(
            jax.ShapeDtypeStruct((block, width), bf16),
            jax.ShapeDtypeStruct((block, width), bf16),
            jax.ShapeDtypeStruct((1, block), f32),
        ),
        in_specs=[vmem] * 4,
        out_specs=(vmem,) * 3,
        scratch_shapes=[
            pltpu.VMEM(chunk, bf16),
            pltpu.VMEM(chunk, bf16),
            pltpu.VMEM((2 * n, ROWS, block), bf16),
            pltpu.VMEM((2 * n, ROWS, block), bf16),
            pltpu.VMEM(chunk, bf16),
            pltpu.VMEM(chunk, bf16),
            pltpu.VMEM(chunk, bf16),
            pltpu.VMEM(chunk, bf16),
            pltpu.VMEM((n, 1, block), f32),
            pltpu.VMEM((1, (n + 1) * block), f32),
            pltpu.VMEM((block // 2, (n + 1) * block), bf16),
            pltpu.VMEM(chunk, f32),
            pltpu.VMEM((block, n * ROWS), bf16),
            pltpu.VMEM((block, (n + 1) * block), f32),
            pltpu.VMEM((width, block), f32),
            pltpu.VMEM((n, 1, block), f32),
            pltpu.VMEM((n, 1, block), f32),
            pltpu.VMEM((1, block), f32),
            pltpu.VMEM((1, block), f32),
        ]
        + [dma((n,))] * 12
        + [dma, dma],
        compiler_params=pltpu.CompilerParams(
            collective_id=0, has_side_effects=True, vmem_limit_bytes=48 * 1024 * 1024
        ),
    )(signal, gating, filter_taps.astype(f32).reshape(1, block), cotangent)
    return (grad_signal, grad_gating, grad_taps.reshape(block))


def solution(mesh):
    in_specs = (P("ctx", "ch"), P("ctx", "ch"), P("ctx"), P("ctx", "ch"))
    out_specs = (P("ctx", "ch"), P("ctx", "ch"), P("ctx"))
    return jax.shard_map(body, mesh=mesh, in_specs=in_specs, out_specs=out_specs, check_vma=False)
```

```python
import functools
import math

import jax
import jax.numpy as jnp
from jax import lax
from jax.experimental import pallas as pl
from jax.experimental.pallas import tpu as pltpu
from jax.sharding import PartitionSpec as P

ROWS = 16
LONG = 24
f32 = jnp.float32
bf16 = jnp.bfloat16


def kernel(
    n, cpd, norm,
    signal_hbm, gating_hbm, taps_hbm, cot_hbm,
    gs_ref, gg_ref, gt_ref,
    signal_ref, gating_ref, taps_ref, cot_ref,
    vsend, gsend, vrecv, xpad, gpad, ysend, bsend, yret, bret,
    hpad, toep, acc, xt_ref, mlag, merge, lagsum, lagother,
    s_v, r_v, s_g, r_g, s_y, r_y, s_b, r_b, s_c, r_c, s_in,
):
    block, width = signal_ref.shape
    total = n * ROWS
    me = lax.axis_index("ctx")
    mate = 1 - lax.axis_index("ch")
    pieces = lax.axis_size("ch")

    barrier = pltpu.get_barrier_semaphore()
    fetches = [
        pltpu.make_async_copy(src, dst, s_in.at[i])
        for i, (src, dst) in enumerate(
            ((signal_hbm, signal_ref), (taps_hbm, taps_ref), (cot_hbm, cot_ref), (gating_hbm, gating_ref))
        )
    ]
    for fetch in fetches:
        fetch.start()

    def greet(d, _):
        pl.semaphore_signal(barrier, inc=1, device_id={"ctx": lax.rem(me + d, n)})
        return 0

    lax.fori_loop(1, n, greet, 0)
    if pieces == 2:
        pl.semaphore_signal(barrier, inc=1, device_id={"ch": mate})

    def split(rows_value, dst):
        if cpd == ROWS:
            dst[:, :ROWS, :] = rows_value.astype(bf16).reshape(n, ROWS, block)
        else:
            for p in range(n):
                part = rows_value[p * cpd : (p + 1) * cpd]
                pad = jnp.zeros((ROWS - cpd, block), f32)
                dst[p, :ROWS, :] = jnp.concatenate([part, pad], axis=0).astype(bf16)

    def joined(src):
        if cpd == ROWS:
            return src[:, :ROWS, :].reshape(width, block).astype(f32)
        for p in range(n):
            merge[p * cpd : (p + 1) * cpd, :] = src[p, :ROWS, :].astype(f32)[:cpd]
        return merge[...]

    def copy(src, dst, send, recv, p, where):
        return pltpu.make_async_remote_copy(
            src_ref=src, dst_ref=dst, send_sem=send.at[p], recv_sem=recv.at[where],
            device_id={"ctx": p},
        )

    def send_all(src, dst, base, send, recv):
        def step(d, _):
            p = lax.rem(me + d, n)
            copy(src.at[p], dst.at[base + me], send, recv, p, me).start()
            return 0

        lax.fori_loop(1, n, step, 0)

    def wait_recv(src, dst, base, send, recv):
        def step(d, _):
            p = lax.rem(me + n - d, n)
            copy(src.at[p], dst.at[base + p], send, recv, p, p).wait_recv()
            return 0

        lax.fori_loop(1, n, step, 0)

    def wait_send(src, dst, base, send, recv):
        def step(d, _):
            p = lax.rem(me + d, n)
            copy(src.at[p], dst.at[base + me], send, recv, p, me).wait_send()
            return 0

        lax.fori_loop(1, n, step, 0)

    fetches[0].wait()
    split(signal_ref[...].astype(f32).T, vsend)
    fetches[1].wait()
    own_taps = taps_ref[...].astype(f32).reshape(1, block)
    vsend[:, ROWS:, :] = jnp.broadcast_to(own_taps.astype(bf16)[None], (n, LONG - ROWS, block))
    pl.semaphore_wait(barrier, n - 1 + (pieces - 1))
    send_all(vsend, vrecv, 0, s_v, r_v)
    fetches[2].wait()
    fetches[3].wait()
    grad_mid = (cot_ref[...].astype(f32) * gating_ref[...].astype(f32)).astype(bf16)
    split(grad_mid.astype(f32).T, gsend)
    send_all(gsend, gpad, 0, s_g, r_g)

    vrecv[pl.ds(me, 1)] = vsend[pl.ds(me, 1)]
    gpad[pl.ds(me, 1)] = gsend[pl.ds(me, 1)]
    gpad[n:] = jnp.zeros((n, ROWS, block), bf16)
    if n > 16:
        xpad[:n] = jnp.zeros((n, ROWS, block), bf16)
    wait_recv(vsend, vrecv, 0, s_v, r_v)
    xpad[n:] = vrecv[:, :ROWS, :]

    half = block // 2
    hpad[:, :block] = jnp.zeros((1, block), f32)
    for j in range(n):
        hpad[:, (j + 1) * block : (j + 2) * block] = vrecv[j, ROWS:, :].astype(f32)[:1]
    toep[:, :block] = jnp.zeros((half, block), bf16)
    for j in range(1, n + 1):
        window = jnp.broadcast_to(hpad[:, j * block - half : (j + 1) * block], (half, block + half))
        turned = pltpu.roll(window, 0, 1, stride=1, stride_axis=0)
        toep[:, j * block : (j + 1) * block] = turned[:, half:].astype(bf16)

    def at(k):
        return k * block if isinstance(k, int) else pl.multiple_of(k * block, block)

    def table(k):
        upper = toep[:, pl.ds(at(k) + block, block)]
        lower = toep[:, pl.ds(at(k) + half, block)]
        return jnp.concatenate([upper, lower], axis=0)

    def over_blocks(step):
        if n <= 16:
            for k in range(n):
                step(k)
        else:
            lax.fori_loop(0, n, lambda k, _: (step(k), 0)[1], 0)

    nt = (((1,), (1,)), ((), ()))

    def forward_step(k):
        if isinstance(k, int):
            term = jnp.dot(
                xpad[n : 2 * n - k].reshape(total - k * ROWS, block), table(k),
                preferred_element_type=f32,
            ).reshape(n - k, ROWS, block)
            if k == 0:
                acc[...] = term
            else:
                acc[k:] += term
        else:
            acc[...] += jnp.dot(
                xpad[pl.ds(n - k, n)].reshape(total, block), table(k), preferred_element_type=f32
            ).reshape(n, ROWS, block)

    def backward_step(k):
        if isinstance(k, int):
            term = lax.dot_general(
                gpad[k:n].reshape(total - k * ROWS, block), table(k), nt,
                preferred_element_type=f32,
            ).reshape(n - k, ROWS, block)
            if k == 0:
                acc[...] = term
            else:
                acc[: n - k] += term
        else:
            acc[...] += lax.dot_general(
                gpad[pl.ds(k, n)].reshape(total, block), table(k), nt, preferred_element_type=f32
            ).reshape(n, ROWS, block)

    if n > 16:
        acc[...] = jnp.zeros((n, ROWS, block), f32)
    over_blocks(forward_step)
    ysend[...] = acc[...].astype(bf16)
    send_all(ysend, yret, 0, s_y, r_y)
    yret[pl.ds(me, 1)] = ysend[pl.ds(me, 1)]
    xt_ref[...] = xpad[n:].reshape(total, block).astype(f32).T.astype(bf16)

    wait_recv(gsend, gpad, 0, s_g, r_g)

    def lag_step(k):
        mlag[:, pl.ds(at(k), block)] = jnp.dot(
            xt_ref[...], gpad[pl.ds(k, n)].reshape(total, block), preferred_element_type=f32
        )

    over_blocks(lag_step)
    mlag[:, n * block :] = jnp.zeros((block, block), f32)

    def fold(c):
        start = at(2 * c)
        span = 2 * block + half
        part = mlag[:half, pl.ds(start, span)] + jnp.concatenate(
            [mlag[half:, pl.ds(start + half, 2 * block)], mlag[half:, pl.ds(start + half + 2 * block, half)]],
            axis=1,
        )
        size = half
        while size > 8:
            size //= 2
            part = part[:size] + pltpu.roll(part[size:], span - size, 1)
        while size > 1:
            size //= 2
            part = part + pltpu.roll(pltpu.roll(part, 8 - size, 0), span - size, 1)
        for i in range(2):
            row = part[:1, i * block : (i + 1) * block]
            high = row.astype(bf16).astype(f32)
            tail = jnp.concatenate([high, row - high, jnp.zeros((LONG - ROWS - 2, block), f32)], axis=0)
            bsend[2 * c + i, ROWS:, :] = tail.astype(bf16)

    if n <= 16:
        for c in range(n // 2):
            fold(c)
    else:
        lax.fori_loop(0, n // 2, lambda c, _: (fold(c), 0)[1], 0)

    if n > 16:
        acc[...] = jnp.zeros((n, ROWS, block), f32)
    over_blocks(backward_step)
    bsend[:, :ROWS, :] = acc[...].astype(bf16)
    send_all(bsend, bret, 0, s_b, r_b)
    bret[pl.ds(me, 1)] = bsend[pl.ds(me, 1)]

    wait_recv(ysend, yret, 0, s_y, r_y)
    recomputed = joined(yret).T
    gg_ref[...] = (cot_ref[...].astype(f32) * recomputed).astype(bf16)

    wait_recv(bsend, bret, 0, s_b, r_b)
    lagsum[...] = jnp.sum(jnp.sum(bret[:, ROWS:, :].astype(f32), axis=0), axis=0, keepdims=True)
    if pieces == 2:
        swap = pltpu.make_async_remote_copy(
            src_ref=lagsum, dst_ref=lagother, send_sem=s_c, recv_sem=r_c, device_id={"ch": mate}
        )
        swap.start()

    gs_ref[...] = joined(bret).T.astype(bf16)
    if pieces == 2:
        swap.wait()
        gt_ref[...] = (lagsum[...] + lagother[...]) * norm
    else:
        gt_ref[...] = lagsum[...] * norm
    wait_send(vsend, vrecv, 0, s_v, r_v)
    wait_send(gsend, gpad, 0, s_g, r_g)
    wait_send(ysend, yret, 0, s_y, r_y)
    wait_send(bsend, bret, 0, s_b, r_b)


def store(gs_in, gg_in, gt_in, gs_out, gg_out, gt_out, sems):
    copies = [
        pltpu.make_async_copy(src, dst, sems.at[i])
        for i, (src, dst) in enumerate(((gs_in, gs_out), (gg_in, gg_out), (gt_in, gt_out)))
    ]
    for copy in copies:
        copy.start()
    for copy in copies:
        copy.wait()


def body(signal, gating, filter_taps, cotangent):
    block, width = signal.shape
    n = lax.axis_size("ctx")
    cpd = width // n
    norm = 1.0 / math.sqrt(width * lax.axis_size("ch") * block * n)
    chunk = (n, ROWS, block)
    longer = (n, LONG, block)
    hbm = pl.BlockSpec(memory_space=pltpu.HBM)
    vmem = pl.BlockSpec(memory_space=pltpu.VMEM)
    dma = pltpu.SemaphoreType.DMA
    grad_signal, grad_gating, grad_taps = pl.pallas_call(
        functools.partial(kernel, n, cpd, norm),
        out_shape=(
            jax.ShapeDtypeStruct((block, width), bf16),
            jax.ShapeDtypeStruct((block, width), bf16),
            jax.ShapeDtypeStruct((1, block), f32),
        ),
        in_specs=[hbm] * 4,
        out_specs=(vmem,) * 3,
        scratch_shapes=[
            pltpu.VMEM((block, width), bf16),
            pltpu.VMEM((block, width), bf16),
            pltpu.VMEM((block,), bf16),
            pltpu.VMEM((block, width), bf16),
            pltpu.VMEM(longer, bf16),
            pltpu.VMEM(chunk, bf16),
            pltpu.VMEM(longer, bf16),
            pltpu.VMEM((2 * n, ROWS, block), bf16),
            pltpu.VMEM((2 * n, ROWS, block), bf16),
            pltpu.VMEM(chunk, bf16),
            pltpu.VMEM(longer, bf16),
            pltpu.VMEM(chunk, bf16),
            pltpu.VMEM(longer, bf16),
            pltpu.VMEM((1, (n + 1) * block), f32),
            pltpu.VMEM((block // 2, (n + 1) * block), bf16),
            pltpu.VMEM(chunk, f32),
            pltpu.VMEM((block, n * ROWS), bf16),
            pltpu.VMEM((block, (n + 1) * block), f32),
            pltpu.VMEM((width, block), f32),
            pltpu.VMEM((1, block), f32),
            pltpu.VMEM((1, block), f32),
        ]
        + [dma((n,))] * 8
        + [dma, dma, dma((4,))],
        compiler_params=pltpu.CompilerParams(
            collective_id=0, has_side_effects=True, vmem_limit_bytes=60 * 1024 * 1024
        ),
    )(signal, gating, filter_taps, cotangent)
    grad_signal, grad_gating, grad_taps = pl.pallas_call(
        store,
        out_shape=(
            jax.ShapeDtypeStruct((block, width), bf16),
            jax.ShapeDtypeStruct((block, width), bf16),
            jax.ShapeDtypeStruct((1, block), f32),
        ),
        in_specs=[hbm] * 3,
        out_specs=(hbm,) * 3,
        scratch_shapes=[dma((3,))],
        compiler_params=pltpu.CompilerParams(vmem_limit_bytes=60 * 1024 * 1024),
    )(grad_signal, grad_gating, grad_taps)
    return (grad_signal, grad_gating, grad_taps.reshape(block))


def solution(mesh):
    in_specs = (P("ctx", "ch"), P("ctx", "ch"), P("ctx"), P("ctx", "ch"))
    out_specs = (P("ctx", "ch"), P("ctx", "ch"), P("ctx"))
    return jax.shard_map(body, mesh=mesh, in_specs=in_specs, out_specs=out_specs, check_vma=False)
```

```python
import functools
import math

import jax
import jax.numpy as jnp
from jax import lax
from jax.experimental import pallas as pl
from jax.experimental.pallas import tpu as pltpu
from jax.sharding import PartitionSpec as P

ROWS = 16
LONG = 24
f32 = jnp.float32
bf16 = jnp.bfloat16


def kernel(
    n, cpd, norm,
    signal_hbm, gating_hbm, taps_hbm, cot_hbm,
    gs_ref, gg_ref, gt_ref,
    signal_ref, gating_ref, taps_ref, cot_ref,
    vsend, gsend, vrecv, xpad, gpad, ysend, bsend, yret, bret,
    hpad, toep, acc, xt_ref, mlag, merge, lagsum, lagother,
    s_v, r_v, s_g, r_g, s_y, r_y, s_b, r_b, s_c, r_c, s_in,
):
    block, width = signal_ref.shape
    total = n * ROWS
    me = lax.axis_index("ctx")
    mate = 1 - lax.axis_index("ch")
    pieces = lax.axis_size("ch")

    barrier = pltpu.get_barrier_semaphore()
    fetches = [
        pltpu.make_async_copy(src, dst, s_in.at[i])
        for i, (src, dst) in enumerate(
            ((signal_hbm, signal_ref), (taps_hbm, taps_ref), (cot_hbm, cot_ref), (gating_hbm, gating_ref))
        )
    ]
    for fetch in fetches:
        fetch.start()

    def greet(d, _):
        pl.semaphore_signal(barrier, inc=1, device_id={"ctx": lax.rem(me + d, n)})
        return 0

    lax.fori_loop(1, n, greet, 0)
    if pieces == 2:
        pl.semaphore_signal(barrier, inc=1, device_id={"ch": mate})

    def split(rows_value, dst):
        if cpd == ROWS:
            dst[:, :ROWS, :] = rows_value.astype(bf16).reshape(n, ROWS, block)
        else:
            for p in range(n):
                part = rows_value[p * cpd : (p + 1) * cpd]
                pad = jnp.zeros((ROWS - cpd, block), f32)
                dst[p, :ROWS, :] = jnp.concatenate([part, pad], axis=0).astype(bf16)

    def joined(src):
        if cpd == ROWS:
            return src[:, :ROWS, :].reshape(width, block).astype(f32)
        for p in range(n):
            merge[p * cpd : (p + 1) * cpd, :] = src[p, :ROWS, :].astype(f32)[:cpd]
        return merge[...]

    def copy(src, dst, send, recv, p, where):
        return pltpu.make_async_remote_copy(
            src_ref=src, dst_ref=dst, send_sem=send.at[p], recv_sem=recv.at[where],
            device_id={"ctx": p},
        )

    def send_all(src, dst, base, send, recv):
        def step(d, _):
            p = lax.rem(me + d, n)
            copy(src.at[p], dst.at[base + me], send, recv, p, me).start()
            return 0

        lax.fori_loop(1, n, step, 0)

    def wait_recv(src, dst, base, send, recv):
        def step(d, _):
            p = lax.rem(me + n - d, n)
            copy(src.at[p], dst.at[base + p], send, recv, p, p).wait_recv()
            return 0

        lax.fori_loop(1, n, step, 0)

    def wait_send(src, dst, base, send, recv):
        def step(d, _):
            p = lax.rem(me + d, n)
            copy(src.at[p], dst.at[base + me], send, recv, p, me).wait_send()
            return 0

        lax.fori_loop(1, n, step, 0)

    fetches[0].wait()
    split(signal_ref[...].astype(f32).T, vsend)
    fetches[1].wait()
    own_taps = taps_ref[...].astype(f32).reshape(1, block)
    vsend[:, ROWS:, :] = jnp.broadcast_to(own_taps.astype(bf16)[None], (n, LONG - ROWS, block))
    pl.semaphore_wait(barrier, n - 1 + (pieces - 1))
    send_all(vsend, vrecv, 0, s_v, r_v)
    fetches[2].wait()
    fetches[3].wait()
    grad_mid = (cot_ref[...].astype(f32) * gating_ref[...].astype(f32)).astype(bf16)
    split(grad_mid.astype(f32).T, gsend)
    send_all(gsend, gpad, 0, s_g, r_g)

    vrecv[pl.ds(me, 1)] = vsend[pl.ds(me, 1)]
    gpad[pl.ds(me, 1)] = gsend[pl.ds(me, 1)]
    gpad[n:] = jnp.zeros((n, ROWS, block), bf16)
    if n > 16:
        xpad[:n] = jnp.zeros((n, ROWS, block), bf16)
    wait_recv(vsend, vrecv, 0, s_v, r_v)
    xpad[n:] = vrecv[:, :ROWS, :]

    half = block // 2
    hpad[:, :block] = jnp.zeros((1, block), f32)
    for j in range(n):
        hpad[:, (j + 1) * block : (j + 2) * block] = vrecv[j, ROWS:, :].astype(f32)[:1]
    toep[:, :block] = jnp.zeros((half, block), bf16)
    for j in range(1, n + 1):
        window = jnp.broadcast_to(hpad[:, j * block - half : (j + 1) * block], (half, block + half))
        turned = pltpu.roll(window, 0, 1, stride=1, stride_axis=0)
        toep[:, j * block : (j + 1) * block] = turned[:, half:].astype(bf16)

    def at(k):
        return k * block if isinstance(k, int) else pl.multiple_of(k * block, block)

    def table(k):
        upper = toep[:, pl.ds(at(k) + block, block)]
        lower = toep[:, pl.ds(at(k) + half, block)]
        return jnp.concatenate([upper, lower], axis=0)

    def over_blocks(step):
        if n <= 16:
            for k in range(n):
                step(k)
        else:
            lax.fori_loop(0, n, lambda k, _: (step(k), 0)[1], 0)

    nt = (((1,), (1,)), ((), ()))

    def forward_step(k):
        if isinstance(k, int):
            term = jnp.dot(
                xpad[n : 2 * n - k].reshape(total - k * ROWS, block), table(k),
                preferred_element_type=f32,
            ).reshape(n - k, ROWS, block)
            if k == 0:
                acc[...] = term
            else:
                acc[k:] += term
        else:
            acc[...] += jnp.dot(
                xpad[pl.ds(n - k, n)].reshape(total, block), table(k), preferred_element_type=f32
            ).reshape(n, ROWS, block)

    def backward_step(k):
        if isinstance(k, int):
            term = lax.dot_general(
                gpad[k:n].reshape(total - k * ROWS, block), table(k), nt,
                preferred_element_type=f32,
            ).reshape(n - k, ROWS, block)
            if k == 0:
                acc[...] = term
            else:
                acc[: n - k] += term
        else:
            acc[...] += lax.dot_general(
                gpad[pl.ds(k, n)].reshape(total, block), table(k), nt, preferred_element_type=f32
            ).reshape(n, ROWS, block)

    if n > 16:
        acc[...] = jnp.zeros((n, ROWS, block), f32)
    over_blocks(forward_step)
    ysend[...] = acc[...].astype(bf16)
    send_all(ysend, yret, 0, s_y, r_y)
    yret[pl.ds(me, 1)] = ysend[pl.ds(me, 1)]
    xt_ref[...] = xpad[n:].reshape(total, block).astype(f32).T.astype(bf16)

    wait_recv(gsend, gpad, 0, s_g, r_g)

    def lag_step(k):
        mlag[:, pl.ds(at(k), block)] = jnp.dot(
            xt_ref[...], gpad[pl.ds(k, n)].reshape(total, block), preferred_element_type=f32
        )

    over_blocks(lag_step)
    mlag[:, n * block :] = jnp.zeros((block, block), f32)

    def fold(c):
        start = at(2 * c)
        span = 2 * block + half
        part = mlag[:half, pl.ds(start, span)] + jnp.concatenate(
            [mlag[half:, pl.ds(start + half, 2 * block)], mlag[half:, pl.ds(start + half + 2 * block, half)]],
            axis=1,
        )
        size = half
        while size > 8:
            size //= 2
            part = part[:size] + pltpu.roll(part[size:], span - size, 1)
        while size > 1:
            size //= 2
            part = part + pltpu.roll(pltpu.roll(part, 8 - size, 0), span - size, 1)
        for i in range(2):
            row = part[:1, i * block : (i + 1) * block]
            high = row.astype(bf16).astype(f32)
            tail = jnp.concatenate([high, row - high, jnp.zeros((LONG - ROWS - 2, block), f32)], axis=0)
            bsend[2 * c + i, ROWS:, :] = tail.astype(bf16)

    if n <= 16:
        for c in range(n // 2):
            fold(c)
    else:
        lax.fori_loop(0, n // 2, lambda c, _: (fold(c), 0)[1], 0)

    if n > 16:
        acc[...] = jnp.zeros((n, ROWS, block), f32)
    over_blocks(backward_step)
    bsend[:, :ROWS, :] = acc[...].astype(bf16)
    send_all(bsend, bret, 0, s_b, r_b)
    bret[pl.ds(me, 1)] = bsend[pl.ds(me, 1)]

    wait_recv(ysend, yret, 0, s_y, r_y)
    recomputed = joined(yret).T
    gg_ref[...] = (cot_ref[...].astype(f32) * recomputed).astype(bf16)

    wait_recv(bsend, bret, 0, s_b, r_b)
    lagsum[...] = jnp.sum(jnp.sum(bret[:, ROWS:, :].astype(f32), axis=0), axis=0, keepdims=True)
    if pieces == 2:
        swap = pltpu.make_async_remote_copy(
            src_ref=lagsum, dst_ref=lagother, send_sem=s_c, recv_sem=r_c, device_id={"ch": mate}
        )
        swap.start()

    gs_ref[...] = joined(bret).T.astype(bf16)
    if pieces == 2:
        swap.wait()
        gt_ref[...] = (lagsum[...] + lagother[...]) * norm
    else:
        gt_ref[...] = lagsum[...] * norm
    wait_send(vsend, vrecv, 0, s_v, r_v)
    wait_send(gsend, gpad, 0, s_g, r_g)
    wait_send(ysend, yret, 0, s_y, r_y)
    wait_send(bsend, bret, 0, s_b, r_b)


def store(gs_in, gg_in, gt_in, gs_out, gg_out, gt_out, sems):
    copies = [
        pltpu.make_async_copy(src, dst, sems.at[i])
        for i, (src, dst) in enumerate(((gs_in, gs_out), (gg_in, gg_out), (gt_in, gt_out)))
    ]
    for copy in copies:
        copy.start()
    for copy in copies:
        copy.wait()


def body(signal, gating, filter_taps, cotangent):
    block, width = signal.shape
    n = lax.axis_size("ctx")
    cpd = width // n
    norm = 1.0 / math.sqrt(width * lax.axis_size("ch") * block * n)
    chunk = (n, ROWS, block)
    longer = (n, LONG, block)
    hbm = pl.BlockSpec(memory_space=pltpu.HBM)
    vmem = pl.BlockSpec(memory_space=pltpu.VMEM)
    dma = pltpu.SemaphoreType.DMA
    grad_signal, grad_gating, grad_taps = pl.pallas_call(
        functools.partial(kernel, n, cpd, norm),
        out_shape=(
            jax.ShapeDtypeStruct((block, width), bf16),
            jax.ShapeDtypeStruct((block, width), bf16),
            jax.ShapeDtypeStruct((1, block), f32),
        ),
        in_specs=[hbm] * 4,
        out_specs=(vmem,) * 3,
        scratch_shapes=[
            pltpu.VMEM((block, width), bf16),
            pltpu.VMEM((block, width), bf16),
            pltpu.VMEM((block,), bf16),
            pltpu.VMEM((block, width), bf16),
            pltpu.VMEM(longer, bf16),
            pltpu.VMEM(chunk, bf16),
            pltpu.VMEM(longer, bf16),
            pltpu.VMEM((2 * n, ROWS, block), bf16),
            pltpu.VMEM((2 * n, ROWS, block), bf16),
            pltpu.VMEM(chunk, bf16),
            pltpu.VMEM(longer, bf16),
            pltpu.VMEM(chunk, bf16),
            pltpu.VMEM(longer, bf16),
            pltpu.VMEM((1, (n + 1) * block), f32),
            pltpu.VMEM((block // 2, (n + 1) * block), bf16),
            pltpu.VMEM(chunk, f32),
            pltpu.VMEM((block, n * ROWS), bf16),
            pltpu.VMEM((block, (n + 1) * block), f32),
            pltpu.VMEM((width, block), f32),
            pltpu.VMEM((1, block), f32),
            pltpu.VMEM((1, block), f32),
        ]
        + [dma((n,))] * 8
        + [dma, dma, dma((4,))],
        compiler_params=pltpu.CompilerParams(
            collective_id=0, has_side_effects=True, vmem_limit_bytes=60 * 1024 * 1024
        ),
    )(signal, gating, filter_taps, cotangent)
    grad_signal, grad_gating, grad_taps = pl.pallas_call(
        store,
        out_shape=(
            jax.ShapeDtypeStruct((block, width), bf16),
            jax.ShapeDtypeStruct((block, width), bf16),
            jax.ShapeDtypeStruct((1, block), f32),
        ),
        in_specs=[vmem] * 3,
        out_specs=(hbm,) * 3,
        scratch_shapes=[dma((3,))],
        compiler_params=pltpu.CompilerParams(vmem_limit_bytes=60 * 1024 * 1024),
    )(grad_signal, grad_gating, grad_taps)
    return (grad_signal, grad_gating, grad_taps.reshape(block))


def solution(mesh):
    in_specs = (P("ctx", "ch"), P("ctx", "ch"), P("ctx"), P("ctx", "ch"))
    out_specs = (P("ctx", "ch"), P("ctx", "ch"), P("ctx"))
    return jax.shard_map(body, mesh=mesh, in_specs=in_specs, out_specs=out_specs, check_vma=False)
```
